32 devices in a mesh: dp: 16 (over z, y, x), tensor: 2 (over core).
Axes of the slice: x: 2, y: 2, z: 4, core: 2. Of those that a mesh axis runs over, the one named last changes fastest.
Arguments:
- tokens: bfloat16 [16, 2048, 768], P('dp'), may hold values from -6 to 6
- target: bfloat16 [16, 2048, 768], P('dp'), may hold values from -6 to 6
- lengths: int32 [16], P('dp'), may hold values from 512 to 2048, as said below
- norm1_gain: float32 [768], replicated, may hold values from 0.5 to 1.5
- w_query: bfloat16 [768, 768], P(None, 'tensor'), may hold values from -0.21875 to 0.21875
- w_key: bfloat16 [768, 768], P(None, 'tensor'), may hold values from -0.21875 to 0.21875
- w_value: bfloat16 [768, 768], P(None, 'tensor'), may hold values from -0.21875 to 0.21875
- shift_kernel: float32 [4, 768], P(None, 'tensor'), may hold values from -3 to 3
- decay_rate: float32 [64, 768], P(None, 'tensor'), may hold values from 0.002 to 0.2
- state_coef: float32 [64, 768], P(None, 'tensor'), may hold values from -0.2 to 0.2
- w_out: bfloat16 [768, 768], P('tensor'), may hold values from -0.21875 to 0.21875
- norm2_gain: float32 [768], replicated, may hold values from 0.5 to 1.5
- w_in: bfloat16 [768, 3072], P(None, 'tensor'), may hold values from -0.21875 to 0.21875
- w_down: bfloat16 [3072, 768], P('tensor'), may hold values from -0.109375 to 0.109375
Outputs:
- output: bfloat16 [16, 2048, 768], P('dp', 'tensor')
- loss: float32 [], replicated
- grad_tokens: float32 [16, 2048, 768], P('dp', 'tensor')
- grad_norm1_gain: float32 [768], replicated
- grad_w_query: float32 [768, 768], P('dp', 'tensor')
- grad_w_key: float32 [768, 768], P('dp', 'tensor')
- grad_w_value: float32 [768, 768], P('dp', 'tensor')
- grad_shift_kernel: float32 [4, 768], replicated
- grad_decay_rate: float32 [64, 768], replicated
- grad_state_coef: float32 [64, 768], replicated
- grad_w_out: float32 [768, 768], P('tensor', 'dp')
- grad_norm2_gain: float32 [768], replicated
- grad_w_in: float32 [768, 3072], P('dp', 'tensor')
- grad_w_down: float32 [3072, 768], P('tensor', 'dp')
The draws below stay inside these ranges and needn't reach their ends.
Inputs may be any that keep to these rules, and one draw needn't show every extreme that they name: `lengths`: each sequence's valid tokens are a prefix; some sequence holds exactly 2048.
All inputs are finite; a program needn't handle non-finite values.
Results may differ from the reference program's by a relative error of at most 0.008.
Values may be sent and summed in bfloat16 or wider, within the bound.
No kernel may reach another device: no remote copies, remote signals or barrier semaphores. Data moves between devices by JAX's collectives and lax.ppermute only.
A program may use at most 256 MiB of HBM per device.

```python
import math
import jax
import jax.numpy as jnp
from jax import lax

D = 768
FF = 3072
STATE = 64
SHIFT = 4
L = 2048
MIN_LEN = 512
BLK = 128
SEQS = 16


def draw_lengths(key, part):
    first_key, second_key = jax.random.split(key)
    drawn_lengths = jax.random.randint(first_key, (SEQS,), MIN_LEN, L + 1)
    chosen = jax.random.randint(second_key, (), 0, SEQS)
    return jnp.where(jnp.arange(SEQS) == chosen, L, drawn_lengths).astype(jnp.int32)


def shard_levels(own_key, dims, cuts, least, high):
    level = 1.0
    for dim, parts in cuts:
        steps = jax.random.uniform(jax.random.fold_in(jax.random.fold_in(own_key, 6), dim), (parts,), jnp.float32, least / len(cuts), high / len(cuts))
        level = level * jnp.repeat(jnp.exp(steps), dims[dim] // parts).reshape((-1,) + (1,) * (len(dims) - 1 - dim))
    return level


def gaussian(own_key, extent, deviation, limit, pieces=(), kind=jnp.bfloat16):
    values = deviation * jax.random.normal(own_key, extent, jnp.float32)
    if pieces:
        values = values * shard_levels(own_key, extent, pieces, -0.22, 0.18)
    return jnp.clip(values, -limit, limit).astype(kind)


def setup_inputs(seed: int = 0) -> dict:
    streams_of = jax.random.split(jax.random.key(seed), 15)
    tokens = gaussian(streams_of[0], (SEQS, L, D), 1.0, 6.0, ((0, 16),))
    target = gaussian(streams_of[1], (SEQS, L, D), 1.0, 6.0, ((0, 16),))
    lengths = draw_lengths(jax.random.fold_in(streams_of[14], 71), 0)
    norm1_gain = jnp.clip(1.0 + 0.1 * jax.random.normal(streams_of[3], (D,), jnp.float32), 0.5, 1.5)
    w_query = gaussian(streams_of[4], (D, D), D ** -0.5, 0.21875, ((1, 2),))
    w_key = gaussian(streams_of[5], (D, D), D ** -0.5, 0.21875, ((1, 2),))
    w_value = gaussian(streams_of[6], (D, D), D ** -0.5, 0.21875, ((1, 2),))
    shift_kernel = gaussian(streams_of[7], (SHIFT, D), 0.5, 3.0, ((1, 2),), jnp.float32)
    decay_rate = jnp.clip(jnp.exp(math.log(0.2) - 4.6051702 * jax.random.uniform(streams_of[8], (STATE, D), jnp.float32) ** shard_levels(streams_of[8], (STATE, D), ((1, 2),), -0.2, 0.2)), 0.002, 0.2)
    state_coef = gaussian(streams_of[9], (STATE, D), 0.03, 0.2, ((1, 2),), jnp.float32)
    w_out = gaussian(streams_of[10], (D, D), D ** -0.5, 0.21875, ((0, 2),))
    norm2_gain = jnp.clip(1.0 + 0.1 * jax.random.normal(streams_of[11], (D,), jnp.float32), 0.5, 1.5)
    w_in = gaussian(streams_of[12], (D, FF), D ** -0.5, 0.21875, ((1, 2),))
    w_down = gaussian(streams_of[13], (FF, D), FF ** -0.5, 0.109375, ((0, 2),))
    return {"tokens": tokens, "target": target, "lengths": lengths, "norm1_gain": norm1_gain, "w_query": w_query, "w_key": w_key, "w_value": w_value, "shift_kernel": shift_kernel, "decay_rate": decay_rate, "state_coef": state_coef, "w_out": w_out, "norm2_gain": norm2_gain, "w_in": w_in, "w_down": w_down}


@jax.custom_vjp
def low(v):
    return lax.optimization_barrier(v.astype(jnp.bfloat16)).astype(jnp.float32)

@jax.custom_vjp
def low_back(v):
    return v

def low_keep(v):
    return (low(v), None)

def low_pass(kept, grad):
    return (grad,)

def back_keep(v):
    return (v, None)

def back_low(kept, grad):
    return (low(grad),)
low.defvjp(low_keep, low_pass)
low_back.defvjp(back_keep, back_low)
EPSILON = 1e-05
HIGHEST_PRECISION = lax.Precision.HIGHEST

def normalize(values):
    center = values - lax.optimization_barrier(jnp.mean(values, axis=-1, keepdims=True))
    return center * lax.rsqrt(lax.optimization_barrier(jnp.mean(center * center, axis=-1, keepdims=True)) + EPSILON)

def matmul(left, right):
    return jnp.dot(left, right, precision=HIGHEST_PRECISION)

def shift_mix(key_rows, shift_kernel):
    padded = jnp.pad(key_rows, ((SHIFT - 1, 0), (0, 0)))
    summed = jnp.zeros_like(key_rows)
    for offset in range(SHIFT):
        summed = summed + shift_kernel[offset] * padded[SHIFT - 1 - offset:SHIFT - 1 - offset + L]
    return summed

def make_taps(decay_rate, state_coef):

    def one_block(block_index):
        positions = (block_index * BLK + jnp.arange(BLK)).astype(jnp.float32)
        decays = jnp.exp(-decay_rate[None] * positions[:, None, None])
        return lax.optimization_barrier(jnp.sum(decays * state_coef[None], axis=1))
    return lax.map(jax.checkpoint(one_block), jnp.arange(L // BLK)).reshape(L, D)

def long_conv(kernel, signal):
    spectrum = jnp.fft.rfft(kernel, n=2 * L, axis=0) * jnp.fft.rfft(signal, n=2 * L, axis=0)
    return jnp.fft.irfft(spectrum, n=2 * L, axis=0)[:L]

def layer(seq_in, kernel, params):
    norm1_gain, w_query, w_key, w_value, shift_kernel, decay_rate, state_coef, w_out, norm2_gain, w_in, w_down = params
    first_in = low(normalize(seq_in) * norm1_gain)
    queries = low_back(matmul(first_in, w_query))
    key_rows = low_back(matmul(first_in, w_key))
    value_rows = low_back(matmul(first_in, w_value))
    shifted = shift_mix(key_rows, shift_kernel)
    products = low(shifted * value_rows)
    convolved = low_back(long_conv(kernel, products))
    gated = low(queries * convolved)
    mixed = low_back(matmul(gated, w_out))
    resid = seq_in + mixed
    second_in = low(normalize(resid) * norm2_gain)
    up_values = low_back(matmul(second_in, w_in))
    activated = low(jax.nn.gelu(up_values, approximate=True))
    down_values = low_back(matmul(activated, w_down))
    return resid + down_values

def reference(tokens, target, lengths, norm1_gain, w_query, w_key, w_value, shift_kernel, decay_rate, state_coef, w_out, norm2_gain, w_in, w_down):
    valid_count = jnp.sum(lengths).astype(jnp.float32)
    params = (norm1_gain, w_query.astype(jnp.float32), w_key.astype(jnp.float32), w_value.astype(jnp.float32), shift_kernel, decay_rate, state_coef, w_out.astype(jnp.float32), norm2_gain, w_in.astype(jnp.float32), w_down.astype(jnp.float32))
    inputs = tokens.astype(jnp.float32)
    goals = target.astype(jnp.float32)

    def forward(all_inputs, all_params):
        kernel = low(make_taps(all_params[5], all_params[6]))

        def one_seq(running, element):
            seq_in, seq_goal, seq_length = element
            final = layer(seq_in, kernel, all_params)
            valid = (jnp.arange(L) < seq_length)[:, None]
            error_rows = jnp.where(valid, final - seq_goal, 0.0)
            return (running + jnp.sum(error_rows * error_rows), final)
        return lax.scan(jax.checkpoint(one_seq), jnp.zeros((), jnp.float32), (all_inputs, goals, lengths))
    (loss_sum, finals), pullback = jax.vjp(forward, inputs, params)
    loss_scale = SEQS * L / 2.0 / valid_count
    input_grad, param_grads = pullback((loss_scale, jnp.zeros_like(finals)))
    loss_value = loss_sum / (valid_count * D)
    return (finals.astype(jnp.bfloat16), loss_value, input_grad, param_grads[0], param_grads[1], param_grads[2], param_grads[3], param_grads[4], param_grads[5], param_grads[6], param_grads[7], param_grads[8], param_grads[9], param_grads[10])
```

```python
import math

import jax
import jax.numpy as jnp
import numpy as np
from jax import lax
from jax.experimental import pallas as pl
from jax.experimental.pallas import tpu as pltpu
from jax.sharding import PartitionSpec as P

EPSILON = 1e-05
F32 = jnp.float32
BF16 = jnp.bfloat16
LANES = 128
ROOT = math.sqrt(0.5)
TAP_BLOCK = 16
ROWS = 256
GELU_SCALE = 0.7978845608
GELU_CUBE = 0.044715


def cost(micros):
    return pl.CostEstimate(flops=int(micros * 1e9), transcendentals=0, bytes_accessed=1024)


def after(value, *others):
    return lax.optimization_barrier((value, others))[0]


def normalize(values):
    center = values - jnp.mean(values, axis=-1, keepdims=True)
    inverse = lax.rsqrt(jnp.mean(center * center, axis=-1, keepdims=True) + EPSILON)
    return (center * inverse, inverse)


def normalize_back(gradient, normed, inverse, gain):
    weighted = gradient * gain
    inner_mean = jnp.mean(weighted * normed, axis=-1, keepdims=True)
    return inverse * (weighted - jnp.mean(weighted, axis=-1, keepdims=True) - normed * inner_mean)


def dot(left, right):
    return jnp.dot(left, right, preferred_element_type=F32)


def dot_t(left, right):
    return lax.dot_general(left, right, (((1,), (1,)), ((), ())), preferred_element_type=F32)


def gelu_pair(a):
    square = a * a
    flat = jnp.tanh(a * (GELU_SCALE + (GELU_SCALE * GELU_CUBE) * square))
    half = 0.5 + 0.5 * flat
    bend = (0.5 * a) * (1.0 - flat * flat)
    return (a * half, half + bend * (GELU_SCALE + (3.0 * GELU_SCALE * GELU_CUBE) * square))


def dft_tables(inner):
    turn = 2.0 * math.pi / inner
    grid = np.outer(np.arange(inner), np.arange(inner)) % inner
    cos, sin = np.cos(turn * grid), np.sin(turn * grid)
    forward = np.block([[cos, sin], [-sin, cos]])
    angle = 2.0 * math.pi / (16 * inner) * np.outer(np.arange(inner), np.arange(1, 9))
    twist = np.zeros((inner, LANES))
    twist[:, 0:8] = np.cos(angle)
    twist[:, 8:16] = np.sin(angle)
    return (
        jnp.asarray(forward, BF16),
        jnp.asarray(forward.T, BF16),
        jnp.asarray(twist, F32),
    )


def spread_twist(twist_ref, wide_ref):
    for column in range(16):
        wide_ref[column] = jnp.broadcast_to(
            twist_ref[:, column : column + 1], wide_ref.shape[1:]
        )


def half_points(e0, e1, e2, e3):
    low, high = (e0 + e2, e1 + e3)
    near, far = ((e1 - e3) * ROOT, high * ROOT)
    return (
        low + high,
        (e0 + near, -e2 - far),
        (e0 - e2, e3 - e1),
        (e0 - near, e2 - far),
        low - high,
    )


def turn_by(value, cos, sin):
    return (value[0] * cos + value[1] * sin, value[1] * cos - value[0] * sin)


def forward_points(load, inner, channels, points_ref, wide_ref):
    def step(index, carry):
        row = pl.multiple_of(index * 16, 16)
        for lane in range(0, channels, LANES):
            x = [load(a, row, lane) for a in range(8)]
            even0, even1, even2, even3, even4 = half_points(x[0], x[2], x[4], x[6])
            odd0, odd1, odd2, odd3, odd4 = half_points(x[1], x[3], x[5], x[7])
            odd1 = turn_by(odd1, math.cos(math.pi / 8), math.sin(math.pi / 8))
            odd2 = turn_by(odd2, ROOT, ROOT)
            odd3 = turn_by(odd3, math.cos(3 * math.pi / 8), math.sin(3 * math.pi / 8))
            out = [
                (even1[0] + odd1[0], even1[1] + odd1[1]),
                (even2[0] + odd2[0], even2[1] + odd2[1]),
                (even3[0] + odd3[0], even3[1] + odd3[1]),
                (even4, -odd4),
                (even3[0] - odd3[0], odd3[1] - even3[1]),
                (even2[0] - odd2[0], odd2[1] - even2[1]),
                (even1[0] - odd1[0], odd1[1] - even1[1]),
            ]
            points_ref[pl.ds(row, 16), lane : lane + LANES] = (even0 + odd0).astype(BF16)
            last = even0 - odd0
            for k in range(1, 9):
                cos = wide_ref[k - 1, pl.ds(row, 16), :]
                sin = wide_ref[k + 7, pl.ds(row, 16), :]
                if k < 8:
                    real, imag = turn_by(out[k - 1], cos, sin)
                else:
                    real, imag = (last * cos, -last * sin)
                at = k * channels + lane
                points_ref[pl.ds(row, 16), at : at + LANES] = real.astype(BF16)
                points_ref[pl.ds(inner + row, 16), at : at + LANES] = imag.astype(BF16)
        return carry

    lax.fori_loop(0, inner // 16, step, 0)


def forward_matrix(points_ref, matrix_ref, inner, channels, spec_ref):
    spec_ref[:, 0:channels] = jnp.dot(
        matrix_ref[:, 0:inner], points_ref[0:inner, 0:channels], preferred_element_type=F32
    ).astype(spec_ref.dtype)
    for k in range(1, 9, 2):
        at = slice(k * channels, (k + 2) * channels)
        spec_ref[:, at] = jnp.dot(
            matrix_ref[...], points_ref[:, at], preferred_element_type=F32
        ).astype(spec_ref.dtype)


def spectra_product(left_ref, right_ref, flip_left, inner, channels, points_ref):
    def step(index, carry):
        row = pl.multiple_of(index * 16, 16)
        low = pl.multiple_of(inner + row, 16)
        for lane in range(0, 9 * channels, LANES):
            at = slice(lane, lane + LANES)
            left_real, left_imag = (left_ref[pl.ds(row, 16), at], left_ref[pl.ds(low, 16), at])
            right_real, right_imag = (right_ref[pl.ds(row, 16), at], right_ref[pl.ds(low, 16), at])
            left_real, left_imag = (left_real.astype(F32), left_imag.astype(F32))
            right_real, right_imag = (right_real.astype(F32), right_imag.astype(F32))
            if flip_left:
                real = left_real * right_real + left_imag * right_imag
                imag = left_real * right_imag - left_imag * right_real
            else:
                real = left_real * right_real - left_imag * right_imag
                imag = left_real * right_imag + left_imag * right_real
            points_ref[pl.ds(row, 16), at] = real.astype(BF16)
            points_ref[pl.ds(low, 16), at] = imag.astype(BF16)
        return carry

    lax.fori_loop(0, inner // 16, step, 0)


def inverse_matrix(points_ref, matrix_ref, inner, channels, values_ref):
    values_ref[0:inner, 0:channels] = jnp.dot(
        matrix_ref[0:inner, :], points_ref[:, 0:channels], preferred_element_type=F32
    )
    for k in range(1, 9, 2):
        at = slice(k * channels, (k + 2) * channels)
        values_ref[:, at] = jnp.dot(
            matrix_ref[...], points_ref[:, at], preferred_element_type=F32
        )


def four_points(start, first, second, third, middle):
    sum_real = (first[0] - third[0]) * ROOT
    sum_imag = (first[1] + third[1]) * ROOT
    return (
        start + middle + first[0] + second[0] + third[0],
        start - middle + sum_real - sum_imag - second[1],
        start + middle - first[1] - second[0] + third[1],
        start - middle - sum_real - sum_imag + second[1],
    )


def inverse_points(values_ref, wide_ref, inner, channels, emit):
    scale = 1.0 / (16 * inner)

    def step(index, carry):
        row = pl.multiple_of(index * 16, 16)
        low = pl.multiple_of(inner + row, 16)
        for lane in range(0, channels, LANES):
            turned = []
            for k in range(1, 9):
                at = slice(k * channels + lane, k * channels + lane + LANES)
                real, imag = (values_ref[pl.ds(row, 16), at], values_ref[pl.ds(low, 16), at])
                cos = wide_ref[k - 1, pl.ds(row, 16), :]
                sin = wide_ref[k + 7, pl.ds(row, 16), :]
                if k < 8:
                    turned.append((real * cos - imag * sin, real * sin + imag * cos))
                else:
                    turned.append(real * cos - imag * sin)
            start = values_ref[pl.ds(row, 16), lane : lane + LANES]
            b1, b2, b3, b4, b5, b6, b7, b8 = turned
            add = [(p[0] + q[0], p[1] - q[1]) for p, q in ((b1, b7), (b2, b6), (b3, b5))]
            sub = [(p[0] - q[0], p[1] + q[1]) for p, q in ((b1, b7), (b2, b6), (b3, b5))]
            sub = [
                turn_by(value, math.cos(k * math.pi / 8), -math.sin(k * math.pi / 8))
                for k, value in zip((1, 2, 3), sub)
            ]
            even = four_points((start + b8) * 0.5, add[0], add[1], add[2], b4[0])
            odd = four_points((start - b8) * 0.5, sub[0], sub[1], sub[2], -b4[1])
            emit(row, lane, [part[j] * (2.0 * scale) for j in range(4) for part in (even, odd)])
        return carry

    lax.fori_loop(0, inner // 16, step, 0)


def kernel_spectrum_body(
    rate_ref, coef_ref, matrix_ref, twist_ref, spec_ref, near_ref, far_ref, taps_ref, points_ref, wide_ref
):
    states, unused, channels = rate_ref.shape
    seq_len = taps_ref.shape[0]
    inner = seq_len // 8
    blocks = seq_len // TAP_BLOCK
    spread_twist(twist_ref, wide_ref)
    offsets = lax.broadcasted_iota(jnp.int32, (TAP_BLOCK, channels), 0).astype(F32)
    starts = lax.broadcasted_iota(jnp.int32, (blocks, channels), 0).astype(F32) * float(TAP_BLOCK)

    def fill(n, carry):
        rate = rate_ref[n]
        near_ref[n] = jnp.exp(-rate * offsets)
        far_ref[n] = jnp.exp(-rate * starts) * coef_ref[n]
        return carry

    lax.fori_loop(0, states, fill, 0)

    def group(index, carry):
        start = pl.multiple_of(index * 8, 8)
        for lane in range(0, channels, LANES):
            at = slice(lane, lane + LANES)

            def add_states(n, sums):
                near, far = (near_ref[n, :, at], far_ref[n, pl.ds(start, 8), at])
                return tuple(sums[a] + far[a : a + 1] * near for a in range(8))

            zero = jnp.zeros((TAP_BLOCK, LANES), F32)
            sums = lax.fori_loop(0, states, add_states, (zero,) * 8, unroll=4)
            for a in range(8):
                row = pl.multiple_of((start + a) * TAP_BLOCK, TAP_BLOCK)
                taps_ref[pl.ds(row, TAP_BLOCK), at] = sums[a]
        return carry

    lax.fori_loop(0, blocks // 8, group, 0)

    def load(a, row, lane):
        rows = taps_ref[pl.ds(a * inner + row, 16), lane : lane + LANES]
        return rows.astype(BF16).astype(F32)

    forward_points(load, inner, channels, points_ref, wide_ref)
    forward_matrix(points_ref, matrix_ref, inner, channels, spec_ref)


def kernel_spectrum(decay_rate, state_coef, matrix, twist, seq_len):
    states, channels = decay_rate.shape
    inner = seq_len // 8
    return pl.pallas_call(
        kernel_spectrum_body,
        out_shape=jax.ShapeDtypeStruct((2 * inner, 9 * channels), BF16),
        scratch_shapes=[
            pltpu.VMEM((states, TAP_BLOCK, channels), F32),
            pltpu.VMEM((states, seq_len // TAP_BLOCK, channels), F32),
            pltpu.VMEM((seq_len, channels), F32),
            pltpu.VMEM((2 * inner, 9 * channels), BF16),
            pltpu.VMEM((16, inner, LANES), F32),
        ],
        cost_estimate=cost(30),
        name="kernel_spectrum",
    )(decay_rate[:, None], state_coef[:, None], matrix, twist)


def conv_body(
    rank_ref, product_ref, query_ref, kernel_ref, matrix_ref, back_ref, twist_ref,
    spec_ref, conv_ref, gated_ref, other_ref, points_ref, values_ref, wide_ref,
):
    seq_len, channels = product_ref.shape
    inner = seq_len // 8
    first = rank_ref[0] == 0
    spread_twist(twist_ref, wide_ref)

    def load(a, row, lane):
        return product_ref[pl.ds(a * inner + row, 16), lane : lane + LANES].astype(F32)

    forward_points(load, inner, channels, points_ref, wide_ref)
    forward_matrix(points_ref, matrix_ref, inner, channels, spec_ref)
    spectra_product(kernel_ref, spec_ref, False, inner, channels, points_ref)
    inverse_matrix(points_ref, back_ref, inner, channels, values_ref)

    def emit(row, lane, values):
        at = slice(lane, lane + LANES)
        gated = []
        for a, value in enumerate(values):
            rows = pl.ds(a * inner + row, 16)
            conv_ref[rows, at] = value
            gated.append(value * query_ref[rows, at])
            gated_ref[rows, at] = gated[a].astype(BF16)
        for a in range(4):
            rows = pl.ds(a * inner + row, 16)
            other_ref[rows, at] = jnp.where(first, gated[a + 4], gated[a]).astype(BF16)

    inverse_points(values_ref, wide_ref, inner, channels, emit)


def whole():
    return pl.BlockSpec(memory_space=pltpu.VMEM)


def convolve(rank, products, queries, kernel_spec, matrix, back, twist):
    seq_len, channels = products.shape
    inner = seq_len // 8
    return pl.pallas_call(
        conv_body,
        in_specs=[pl.BlockSpec(memory_space=pltpu.SMEM)] + [whole()] * 6,
        out_shape=(
            jax.ShapeDtypeStruct((2 * inner, 9 * channels), BF16),
            jax.ShapeDtypeStruct((seq_len, channels), F32),
            jax.ShapeDtypeStruct((seq_len, channels), BF16),
            jax.ShapeDtypeStruct((seq_len // 2, channels), BF16),
        ),
        scratch_shapes=[
            pltpu.VMEM((2 * inner, 9 * channels), BF16),
            pltpu.VMEM((2 * inner, 9 * channels), F32),
            pltpu.VMEM((16, inner, LANES), F32),
        ],
        cost_estimate=cost(19),
        name="convolve",
    )(rank, products, queries, kernel_spec, matrix, back, twist)


def conv_back_body(
    rank_ref, own_grad_ref, swap_grad_ref, query_ref, conv_ref, key_ref, value_ref, shifted_ref, shift_ref,
    kernel_ref, spec_ref, matrix_ref, back_ref, twist_ref,
    mixed_ref, shift_grad_ref, kernel_grad_ref,
    grad_spec_ref, points_ref, values_ref, wide_ref, ahead_ref,
):
    seq_len, channels = query_ref.shape
    inner = seq_len // 8
    taps = shift_ref.shape[0]
    first = rank_ref[0] == 0
    spread_twist(twist_ref, wide_ref)

    def load(a, row, lane):
        at = slice(lane, lane + LANES)
        near = pl.ds((a % 4) * inner + row, 16)
        rows = pl.ds(a * inner + row, 16)
        own, other = (own_grad_ref[near, at], swap_grad_ref[near, at])
        own, other = (own.astype(F32), other.astype(F32))
        grad = jnp.where(first, own, other) if a < 4 else jnp.where(first, other, own)
        mixed_ref[rows, at] = (grad * conv_ref[rows, at]).astype(BF16)
        return (grad * query_ref[rows, at]).astype(BF16).astype(F32)

    forward_points(load, inner, channels, points_ref, wide_ref)
    forward_matrix(points_ref, matrix_ref, inner, channels, grad_spec_ref)
    spectra_product(kernel_ref, grad_spec_ref, True, inner, channels, points_ref)
    inverse_matrix(points_ref, back_ref, inner, channels, values_ref)

    def emit_product(row, lane, values):
        at = slice(lane, lane + LANES)
        late = slice(2 * channels + lane, 2 * channels + lane + LANES)
        for a, value in enumerate(values):
            rows = pl.ds(a * inner + row, 16)
            mixed_ref[rows, late] = (value * shifted_ref[rows, at].astype(F32)).astype(BF16)
            ahead_ref[rows, at] = value * value_ref[rows, at].astype(F32)

    inverse_points(values_ref, wide_ref, inner, channels, emit_product)
    ahead_ref[pl.ds(seq_len, 8), :] = jnp.zeros((8, channels), F32)

    for lane in range(0, channels, LANES):
        at = slice(lane, lane + LANES)
        middle = slice(channels + lane, channels + lane + LANES)

        def shift_step(index, sums):
            row = pl.multiple_of(index * 32, 32)
            grads = ahead_ref[pl.ds(row, 40), at]
            before = pl.multiple_of(jnp.maximum(row - 16, 0), 16)
            past = key_ref[pl.ds(before, 16), at].astype(F32) * jnp.where(index > 0, 1.0, 0.0)
            keys = jnp.concatenate((past, key_ref[pl.ds(row, 32), at].astype(F32)), axis=0)
            total = shift_ref[0:1, at] * grads[0:32]
            for j in range(1, taps):
                total = total + shift_ref[j : j + 1, at] * grads[j : j + 32]
            mixed_ref[pl.ds(row, 32), middle] = total.astype(BF16)
            return tuple(
                sums[j] + grads[0:32] * keys[16 - j : 48 - j] for j in range(taps)
            )

        zero = jnp.zeros((32, LANES), F32)
        sums = lax.fori_loop(0, seq_len // 32, shift_step, (zero,) * taps)
        for j in range(taps):
            shift_grad_ref[j : j + 1, at] = jnp.sum(sums[j], axis=0, keepdims=True)

    spectra_product(spec_ref, grad_spec_ref, True, inner, channels, points_ref)
    inverse_matrix(points_ref, back_ref, inner, channels, values_ref)

    def emit_kernel(row, lane, values):
        for a, value in enumerate(values):
            kernel_grad_ref[pl.ds(a * inner + row, 16), lane : lane + LANES] = value

    inverse_points(values_ref, wide_ref, inner, channels, emit_kernel)


def convolve_back(rank, grads, rows, shift_kernel, specs, tables):
    seq_len, channels = rows[0].shape
    inner = seq_len // 8
    operands = (*grads, *rows, shift_kernel, *specs, *tables)
    return pl.pallas_call(
        conv_back_body,
        in_specs=[pl.BlockSpec(memory_space=pltpu.SMEM)] + [whole()] * len(operands),
        out_shape=(
            jax.ShapeDtypeStruct((seq_len, 3 * channels), BF16),
            jax.ShapeDtypeStruct(shift_kernel.shape, F32),
            jax.ShapeDtypeStruct((seq_len, channels), F32),
        ),
        scratch_shapes=[
            pltpu.VMEM((2 * inner, 9 * channels), F32),
            pltpu.VMEM((2 * inner, 9 * channels), BF16),
            pltpu.VMEM((2 * inner, 9 * channels), F32),
            pltpu.VMEM((16, inner, LANES), F32),
            pltpu.VMEM((seq_len + 8, channels), F32),
        ],
        cost_estimate=cost(28),
        name="convolve_back",
    )(rank, *operands)


def front_body(
    token_ref, gain_ref, query_w_ref, key_w_ref, value_w_ref, shift_ref,
    first_ref, query_ref, key_ref, value_ref, shifted_ref, product_ref, past_ref,
):
    @pl.when(pl.program_id(0) == 0)
    def _():
        past_ref[...] = jnp.zeros(past_ref.shape, F32)

    rows = token_ref.shape[0]
    first = (normalize(token_ref[...].astype(F32))[0] * gain_ref[...]).astype(BF16)
    first_ref[...] = first
    query_ref[...] = dot(first, query_w_ref[...])
    keys = dot(first, key_w_ref[...])
    values = dot(first, value_w_ref[...])
    long = jnp.concatenate((past_ref[...], keys), axis=0)
    past_ref[...] = keys[rows - 8 :]
    shifted = shift_ref[0:1] * keys
    for j in range(1, shift_ref.shape[0]):
        shifted = shifted + shift_ref[j : j + 1] * long[8 - j : 8 - j + rows]
    key_ref[...] = keys.astype(BF16)
    value_ref[...] = values.astype(BF16)
    shifted_ref[...] = shifted.astype(BF16)
    product_ref[...] = (shifted * values).astype(BF16)


def fixed(shape):
    return pl.BlockSpec(shape, lambda *_: (0,) * len(shape), pipeline_mode=pl.Buffered(1))


def front(tokens, gain, w_query, w_key, w_value, shift_kernel):
    seq_len, width = tokens.shape
    channels = w_query.shape[1]

    def rows(columns):
        return pl.BlockSpec((ROWS, columns), lambda i: (i, 0))

    weight = fixed((width, channels))
    kinds = (F32, BF16, BF16, BF16, BF16)
    return pl.pallas_call(
        front_body,
        grid=(seq_len // ROWS,),
        in_specs=[rows(width), fixed((1, width)), weight, weight, weight, fixed(shift_kernel.shape)],
        out_specs=[rows(width)] + [rows(channels)] * 5,
        out_shape=[jax.ShapeDtypeStruct((seq_len, width), BF16)]
        + [jax.ShapeDtypeStruct((seq_len, channels), kind) for kind in kinds],
        scratch_shapes=[pltpu.VMEM((8, channels), F32)],
        cost_estimate=cost(9),
        name="front",
    )(tokens, gain[None], w_query, w_key, w_value, shift_kernel)


CHUNK = 512


def feed_body(
    rank_ref, gated_ref, swapped_ref, token_ref, target_ref, length_ref, gain_ref,
    out_own_ref, out_swap_ref, in_own_ref, in_swap_ref, down_own_ref, down_swap_ref,
    final_ref, second_ref, normed_ref, inverse_ref, error_ref, grad_ref,
    act_own_ref, act_swap_ref, slope_own_ref, slope_swap_ref, loss_ref,
):
    step = pl.program_id(0)
    rows = token_ref.shape[0]
    mixed = dot(gated_ref[...], out_own_ref[...]) + dot(swapped_ref[...], out_swap_ref[...])
    resid = token_ref[...].astype(F32) + mixed
    normed, inverse = normalize(resid)
    second = (normed * gain_ref[...]).astype(BF16)
    normed_ref[...] = normed
    inverse_ref[...] = jnp.broadcast_to(inverse, inverse_ref.shape)
    second_ref[...] = second
    final = resid
    for in_ref, down_ref, act_ref, slope_ref in (
        (in_own_ref, down_own_ref, act_own_ref, slope_own_ref),
        (in_swap_ref, down_swap_ref, act_swap_ref, slope_swap_ref),
    ):
        for start in range(0, in_ref.shape[1], CHUNK):
            at = slice(start, start + CHUNK)
            act, slope = gelu_pair(dot(second, in_ref[:, at]))
            act = act.astype(BF16)
            act_ref[:, at] = act
            slope_ref[:, at] = slope.astype(BF16)
            final = final + dot(act, down_ref[at, :])
    final_ref[...] = final.astype(BF16)
    place = (rank_ref[0] * pl.num_programs(0) + step) * rows
    place = place + lax.broadcasted_iota(jnp.int32, final.shape, 0)
    error = jnp.where(place < length_ref[0], final - target_ref[...].astype(F32), 0.0)
    error_ref[...] = error
    grad_ref[...] = error.astype(BF16)

    @pl.when(step == 0)
    def _():
        loss_ref[...] = jnp.zeros(loss_ref.shape, F32)

    square = error * error
    loss_ref[...] += jnp.sum(square.reshape(rows // 8, 8, square.shape[1]), axis=0)


def feed(rank, gated, swapped, tokens, target, lengths, gain, weights):
    half, channels = swapped.shape
    width = tokens.shape[1]
    hidden = weights[2].shape[1]
    steps = half // ROWS

    def own(columns):
        return pl.BlockSpec((ROWS, columns), lambda i, rank: (rank[0] * steps + i, 0))

    def rows(columns):
        return pl.BlockSpec((ROWS, columns), lambda i, rank: (i, 0))

    def shape(columns, kind):
        return jax.ShapeDtypeStruct((half, columns), kind)

    wide = (width, width, width, LANES, width, width, hidden, hidden, hidden, hidden)
    kinds = (BF16, BF16, F32, F32, F32, BF16, BF16, BF16, BF16, BF16)
    return pl.pallas_call(
        feed_body,
        grid_spec=pltpu.PrefetchScalarGridSpec(
            num_scalar_prefetch=1,
            grid=(steps,),
            in_specs=[
                own(channels), rows(channels), own(width), own(width),
                pl.BlockSpec(memory_space=pltpu.SMEM), fixed((1, width)),
            ]
            + [fixed(weight.shape) for weight in weights],
            out_specs=[rows(columns) for columns in wide]
            + [pl.BlockSpec((8, width), lambda i, rank: (0, 0))],
        ),
        out_shape=[shape(columns, kind) for columns, kind in zip(wide, kinds)]
        + [jax.ShapeDtypeStruct((8, width), F32)],
        cost_estimate=cost(22),
        name="feed",
    )(rank, gated, swapped, tokens, target, lengths, gain[None], *weights)


def feed_back_body(
    grad_ref, slope_own_ref, slope_swap_ref, normed_ref, inverse_ref, error_ref, gain_ref,
    out_own_ref, out_swap_ref, in_own_ref, in_swap_ref, down_own_ref, down_swap_ref,
    up_own_ref, up_swap_ref, mixer_ref, resid_ref, gated_own_ref, gated_swap_ref, gain_grad_ref,
):
    step = pl.program_id(0)
    rows = grad_ref.shape[0]
    grad = grad_ref[...]
    second = jnp.zeros(normed_ref.shape, F32)
    for in_ref, down_ref, slope_ref, up_ref in (
        (in_own_ref, down_own_ref, slope_own_ref, up_own_ref),
        (in_swap_ref, down_swap_ref, slope_swap_ref, up_swap_ref),
    ):
        for start in range(0, in_ref.shape[1], CHUNK):
            at = slice(start, start + CHUNK)
            up = (dot_t(grad, down_ref[at, :]) * slope_ref[:, at].astype(F32)).astype(BF16)
            up_ref[:, at] = up
            second = second + dot_t(up, in_ref[:, at])
    normed = normed_ref[...]

    @pl.when(step == 0)
    def _():
        gain_grad_ref[...] = jnp.zeros(gain_grad_ref.shape, F32)

    gain_part = second * normed
    gain_grad_ref[...] += jnp.sum(gain_part.reshape(rows // 8, 8, gain_part.shape[1]), axis=0)
    resid = error_ref[...] + normalize_back(second, normed, inverse_ref[:, 0:1], gain_ref[...])
    resid_ref[...] = resid
    mixer = resid.astype(BF16)
    mixer_ref[...] = mixer
    gated_own_ref[...] = dot_t(mixer, out_own_ref[...]).astype(BF16)
    gated_swap_ref[...] = dot_t(mixer, out_swap_ref[...]).astype(BF16)


def feed_back(grad, slopes, normed, inverse, error, gain, weights):
    half, width = grad.shape
    channels, hidden = (weights[0].shape[0], weights[2].shape[1])

    def rows(columns):
        return pl.BlockSpec((ROWS, columns), lambda i: (i, 0))

    wide = (hidden, hidden, width, width, channels, channels)
    kinds = (BF16, BF16, BF16, F32, BF16, BF16)
    return pl.pallas_call(
        feed_back_body,
        grid=(half // ROWS,),
        in_specs=[
            rows(width), rows(hidden), rows(hidden), rows(width), rows(LANES), rows(width),
            fixed((1, width)),
        ]
        + [fixed(weight.shape) for weight in weights],
        out_specs=[rows(columns) for columns in wide] + [pl.BlockSpec((8, width), lambda i: (0, 0))],
        out_shape=[jax.ShapeDtypeStruct((half, columns), kind) for columns, kind in zip(wide, kinds)]
        + [jax.ShapeDtypeStruct((8, width), F32)],
        cost_estimate=cost(22),
        name="feed_back",
    )(grad, *slopes, normed, inverse, error, gain[None], *weights)


def first_back_body(
    rank_ref, mixed_ref, token_ref, query_w_ref, key_w_ref, value_w_ref, other_ref, own_ref, gain_ref
):
    step = pl.program_id(0)
    rows, channels = (mixed_ref.shape[0], query_w_ref.shape[1])
    part = dot_t(mixed_ref[:, :channels], query_w_ref[...])
    part = part + dot_t(mixed_ref[:, channels : 2 * channels], key_w_ref[...])
    part = part + dot_t(mixed_ref[:, 2 * channels :], value_w_ref[...])
    normed = normalize(token_ref[...].astype(F32))[0]

    @pl.when(step == 0)
    def _():
        gain_ref[...] = jnp.zeros(gain_ref.shape, F32)

    gain_part = part * normed
    gain_ref[...] += jnp.sum(gain_part.reshape(rows // 8, 8, gain_part.shape[1]), axis=0)
    steps = pl.num_programs(0) // 2

    @pl.when(step < steps)
    def _():
        other_ref[...] = part.astype(BF16)

    @pl.when(step >= steps)
    def _():
        own_ref[...] = part


def first_back(rank, mixed_grad, tokens, w_query, w_key, w_value):
    seq_len, width = tokens.shape
    steps = seq_len // (2 * ROWS)

    def rows(columns):
        def place(i, rank):
            side = jnp.where(i < steps, 1 - rank[0], rank[0])
            return (side * steps + i % steps, 0)

        return pl.BlockSpec((ROWS, columns), place)

    weight = fixed(w_query.shape)
    return pl.pallas_call(
        first_back_body,
        grid_spec=pltpu.PrefetchScalarGridSpec(
            num_scalar_prefetch=1,
            grid=(2 * steps,),
            in_specs=[rows(mixed_grad.shape[1]), rows(width), weight, weight, weight],
            out_specs=[
                pl.BlockSpec((ROWS, width), lambda i, rank: (jnp.minimum(i, steps - 1), 0)),
                pl.BlockSpec((ROWS, width), lambda i, rank: (jnp.maximum(i - steps, 0), 0)),
                pl.BlockSpec((8, width), lambda i, rank: (0, 0)),
            ],
        ),
        out_shape=[
            jax.ShapeDtypeStruct((seq_len // 2, width), BF16),
            jax.ShapeDtypeStruct((seq_len // 2, width), F32),
            jax.ShapeDtypeStruct((8, width), F32),
        ],
        cost_estimate=cost(9),
        name="first_back",
    )(rank, mixed_grad, tokens, w_query, w_key, w_value)


def last_body(rank_ref, own_ref, swapped_ref, token_ref, resid_ref, gain_ref, scale_ref, out_ref):
    grad = own_ref[...] + swapped_ref[...].astype(F32)
    normed, inverse = normalize(token_ref[...].astype(F32))
    total = resid_ref[...] + normalize_back(grad, normed, inverse, gain_ref[...])
    out_ref[...] = total * scale_ref[0]


def last(rank, own_part, swapped, tokens, resid_grad, gain, scale):
    half, width = own_part.shape
    steps = half // ROWS
    rows = pl.BlockSpec((ROWS, width), lambda i, rank: (i, 0))
    own = pl.BlockSpec((ROWS, width), lambda i, rank: (rank[0] * steps + i, 0))
    return pl.pallas_call(
        last_body,
        grid_spec=pltpu.PrefetchScalarGridSpec(
            num_scalar_prefetch=1,
            grid=(steps,),
            in_specs=[
                rows, rows, own, rows, fixed((1, width)), pl.BlockSpec(memory_space=pltpu.SMEM),
            ],
            out_specs=rows,
        ),
        out_shape=jax.ShapeDtypeStruct((half, width), F32),
        cost_estimate=cost(5),
        name="last",
    )(rank, own_part, swapped, tokens, resid_grad, gain[None], scale)


def taps_back_body(kernel_grad_ref, rate_ref, coef_ref, rate_grad_ref, coef_grad_ref):
    half = kernel_grad_ref.shape[0] // 2
    rate = rate_ref[...]
    decay = jnp.exp(-rate)

    def step(index, sums):
        low, low_slope, high, high_slope = sums
        row = half - 8 - index * 8
        low_rows = kernel_grad_ref[pl.ds(pl.multiple_of(row, 8), 8), :]
        high_rows = kernel_grad_ref[pl.ds(pl.multiple_of(half + row, 8), 8), :]
        for r in range(7, -1, -1):
            low_slope = low_slope * decay + low
            low = low * decay + low_rows[r : r + 1]
            high_slope = high_slope * decay + high
            high = high * decay + high_rows[r : r + 1]
        return (low, low_slope, high, high_slope)

    zero = jnp.zeros(rate.shape, F32)
    low, low_slope, high, high_slope = lax.fori_loop(0, half // 8, step, (zero,) * 4)
    reach = jnp.exp(-rate * float(half))
    coef_grad_ref[...] = low + reach * high
    slope = decay * low_slope + reach * (float(half) * high + decay * high_slope)
    rate_grad_ref[...] = -coef_ref[...] * slope


def taps_back(kernel_grad, decay_rate, state_coef, tile):
    seq_len, states = (kernel_grad.shape[0], decay_rate.shape[0])

    def pick(rows):
        return pl.BlockSpec((rows, LANES), lambda i: (0, tile))

    out = pl.BlockSpec((states, LANES), lambda i: (0, 0))
    return pl.pallas_call(
        taps_back_body,
        grid=(1,),
        in_specs=[pick(seq_len), pick(states), pick(states)],
        out_specs=(out, out),
        out_shape=(jax.ShapeDtypeStruct((states, LANES), F32),) * 2,
        cost_estimate=cost(11),
        name="taps_back",
    )(kernel_grad, decay_rate, state_coef)


def swap(piece):
    return lax.ppermute(piece, "tensor", [(0, 1), (1, 0)])


def cross(piece, mask):
    size = lax.axis_size("dp")
    return lax.ppermute(piece, "dp", [(i, i ^ mask) for i in range(size)])


def dp_phases():
    bits = list(range(lax.axis_size("dp").bit_length() - 1))
    return [tuple(bits[i : i + 2]) for i in range(0, len(bits), 2)]


def masks_of(phase):
    return [sum(((m >> j) & 1) << bit for j, bit in enumerate(phase)) for m in range(1 << len(phase))]


class RowSum:
    def __init__(self):
        self.phases = dp_phases()
        self.left = [bit for phase in self.phases for bit in phase][::-1]
        self.terms = self.kept = None
        self.away, self.got = ([], [])

    def load(self, *terms):
        bits = len(self.left)
        rows = terms[0].shape[0] >> bits
        self.terms = [term.reshape((2,) * bits + (rows,) + term.shape[1:]) for term in terms]
        return self

    def load_pair(self, own, other):
        self.kept, self.away, self.got = (own, [other], [swap(other)])
        return self

    def collect(self):
        if self.got:
            terms, self.got = ([self.kept] + self.got, [])
            if self.terms is None:
                self.load(*terms)
            else:
                self.terms = terms
        return self.terms

    def step(self):
        terms = self.collect()
        if not self.phases:
            return
        phase = self.phases.pop(0)
        index = lax.axis_index("dp")

        def pick(term, mask):
            start, size, rest = ([], [], [])
            for bit, extent in zip(self.left, term.shape):
                start.append(((index ^ mask) >> bit) & 1 if bit in phase else 0)
                size.append(1 if bit in phase else extent)
                rest += [] if bit in phase else [extent]
            tail = list(term.shape[len(self.left) :])
            piece = lax.dynamic_slice(term, start + [0] * len(tail), size + tail)
            return piece.reshape(rest + tail).astype(F32)

        masks = masks_of(phase)
        pieces = [sum(pick(term, mask) for term in terms) for mask in masks]
        self.left = [bit for bit in self.left if bit not in phase]
        self.kept, self.away = (pieces[0], [piece.astype(BF16) for piece in pieces[1:]])
        self.got = [cross(piece, mask) for piece, mask in zip(self.away, masks[1:])]

    def result(self):
        while self.phases:
            self.step()
        return sum(term.astype(F32) for term in self.collect())


def gate(value, *sums):
    value, got = lax.optimization_barrier((value, [item.got for item in sums]))
    for item, pieces in zip(sums, got):
        item.got = pieces
        item.step()
    return after(value, *[item.away for item in sums])


def settle(value, *sums):
    value, got = lax.optimization_barrier((value, [item.got for item in sums]))
    for item, pieces in zip(sums, got):
        item.got = pieces
    return value


def sum_all(piece):
    for phase in dp_phases():
        piece = piece.astype(BF16)
        masks = masks_of(phase)
        got = [piece] + [cross(piece, mask) for mask in masks[1:]]
        got = [part.astype(F32) for part in got]
        while len(got) > 1:
            got = [got[i] + got[i + 1] for i in range(0, len(got), 2)]
        piece = got[0]
    return piece


def row_product(left, right):
    return jnp.einsum("rd,rc->dc", left, right, preferred_element_type=F32)


def local(
    tokens, target, lengths, norm1_gain, w_query, w_key, w_value, shift_kernel,
    decay_rate, state_coef, w_out, norm2_gain, w_in, w_down,
):
    tokens, target = (tokens[0], target[0])
    seq_len, width = tokens.shape
    channels = w_query.shape[1]
    rank = lax.axis_index("tensor")
    side = rank.astype(jnp.int32).reshape(1)
    tables = dft_tables(seq_len // 8)
    weights = (w_out, swap(w_out), w_in, swap(w_in), w_down, swap(w_down))

    first_in, queries, key_rows, value_rows, shifted_keys, products = front(
        tokens, norm1_gain, w_query, w_key, w_value, shift_kernel
    )
    kernel_spec = kernel_spectrum(decay_rate, state_coef, tables[0], tables[2], seq_len)
    product_spec, convolved, gated, gated_other = convolve(
        side, products, queries, kernel_spec, *tables
    )
    gated_swap = swap(gated_other)
    (
        final_rows, second_in, second_normed, second_inverse, error_rows, down_grad,
        act_own, act_swap, slope_own, slope_swap, loss_part,
    ) = feed(side, gated, gated_swap, tokens, target, lengths, norm2_gain, weights)
    down_t = RowSum().load_pair(
        row_product(down_grad, act_own), row_product(down_grad, act_swap).astype(BF16)
    )
    down_grad = after(gate(down_grad, down_t), down_t.away)
    (
        up_own, up_swap, mixer_grad, resid_grad, gated_own_grad, gated_swap_grad, gain2_grad,
    ) = feed_back(
        down_grad, (slope_own, slope_swap), second_normed, second_inverse, error_rows, norm2_gain, weights
    )
    gated_swap_grad = swap(gated_swap_grad)
    second_in = after(second_in, gated_own_grad)
    up_t = RowSum().load_pair(
        row_product(second_in, up_own), row_product(second_in, up_swap).astype(BF16)
    )
    mixer_grad = after(mixer_grad, up_t.away)
    gated_own = lax.dynamic_slice_in_dim(gated, rank * (seq_len // 2), seq_len // 2, 0)
    out_t = RowSum().load_pair(
        row_product(mixer_grad, gated_own), row_product(mixer_grad, gated_swap).astype(BF16)
    )
    gated_own_grad = after(gate(gated_own_grad, up_t, down_t), out_t.away)
    mixed_grad, shift_grad, kernel_grad = convolve_back(
        side,
        (gated_own_grad, gated_swap_grad),
        (queries, convolved, key_rows, value_rows, shifted_keys),
        shift_kernel,
        (kernel_spec, product_spec),
        tables,
    )
    mixed_grad = gate(mixed_grad, up_t, out_t)
    mixed_grad = settle(mixed_grad, down_t)
    key_t = RowSum().load(row_product(first_in, mixed_grad))
    mixed_grad = gate(mixed_grad, key_t)
    first_other, first_own, gain1_grad = first_back(
        side, mixed_grad, tokens, w_query, w_key, w_value
    )
    first_swap = swap(first_other)
    kernel_grad = after(kernel_grad, first_own)
    pieces = []
    for tile in range(channels // LANES):
        if tile == 0:
            kernel_grad = gate(settle(kernel_grad, up_t), out_t)
        elif tile == 1:
            kernel_grad = gate(after(kernel_grad, pieces[-1]), key_t)
        else:
            kernel_grad = settle(after(kernel_grad, pieces[-1]), out_t)
        pieces.append(taps_back(kernel_grad, decay_rate, state_coef, tile))
    pieces = settle(pieces, key_t)
    rate_grad = jnp.concatenate([piece[0] for piece in pieces], axis=1)
    coef_grad = jnp.concatenate([piece[1] for piece in pieces], axis=1)

    digit_count = seq_len.bit_length()
    column = jnp.arange(channels)
    digits = jnp.where(column < digit_count, (lengths[0] >> jnp.minimum(column, 30)) & 1, 0)
    small = jnp.concatenate(
        (
            rate_grad,
            coef_grad,
            shift_grad,
            jnp.sum(gain1_grad, axis=0).reshape(2, channels),
            jnp.sum(gain2_grad, axis=0).reshape(2, channels),
            jnp.full((1, channels), jnp.sum(loss_part)),
            digits.astype(F32)[None],
            jnp.zeros((6, channels), F32),
        ),
        axis=0,
    )
    small = sum_all(small)
    states, taps = (decay_rate.shape[0], shift_kernel.shape[0])
    split = 2 * states + taps
    powers = jnp.where(column < digit_count, jnp.exp2(column.astype(F32)), 0.0)
    valid_count = jnp.sum(small[split + 5] * powers)
    scale = float(seq_len * lax.axis_size("dp")) / valid_count
    small = small.astype(BF16)
    other = swap(small).astype(F32)
    small = small.astype(F32)
    lead = jnp.where(rank == 0, small[:split], other[:split])
    tail = jnp.where(rank == 0, other[:split], small[:split])
    wide = jnp.concatenate((lead, tail), axis=1) * scale
    gains = (small + other)[split:]
    loss_value = gains[4, 0] / (valid_count * width)
    gains = gains * scale
    input_grad = last(
        side, first_own, first_swap, tokens, resid_grad, norm1_gain, scale.reshape(1)
    )
    key_sum = key_t.result() * scale
    return (
        final_rows[None],
        loss_value,
        input_grad[None],
        gains[0:2].reshape(width),
        key_sum[:, :channels],
        key_sum[:, channels : 2 * channels],
        key_sum[:, 2 * channels :],
        wide[2 * states :],
        wide[:states],
        wide[states : 2 * states],
        (out_t.result() * scale).T,
        gains[2:4].reshape(width),
        up_t.result() * scale,
        (down_t.result() * scale).T,
    )


def solution(mesh):
    rows, columns = (P(None, "tensor"), P("tensor", None))
    sequences = P("dp", None, None)
    halves = P("dp", "tensor", None)
    return jax.shard_map(
        local,
        mesh=mesh,
        in_specs=(
            sequences, sequences, P("dp"), P(), rows, rows, rows, rows,
            rows, rows, columns, P(), rows, columns,
        ),
        out_specs=(
            halves, P(), halves, P(), P("dp", "tensor"), P("dp", "tensor"), P("dp", "tensor"),
            P(), P(), P(), P("tensor", "dp"), P(), P("dp", "tensor"), P("tensor", "dp"),
        ),
        check_vma=False,
    )
```
